32 devices in a mesh: fsdp: 32 (over z, y, x, core).
Axes of the slice: x: 2, y: 2, z: 4, core: 2. Of those that a mesh axis runs over, the one named last changes fastest.
Arguments:
- images: float32 [32, 196, 512], P('fsdp'), may hold values from -40 to 40
- counts: int32 [32], P('fsdp'), may hold values from 0 to 1, as said below
- cotangent: float32 [32, 196, 512], P('fsdp'), may hold values from -40 to 40
- params: float32 [2, 3158016], P(None, 'fsdp'), may hold values from -10 to 240
- first_moment: float32 [2, 3158016], P(None, 'fsdp'), may hold values from -12 to 12
- second_moment: float32 [2, 3158016], P(None, 'fsdp'), may hold values from 1 to 100
Outputs:
- block_out: float32 [32, 196, 512], P('fsdp')
- input_grad: float32 [32, 196, 512], P('fsdp')
- param_grads: float32 [2, 3158016], P(None, 'fsdp')
- new_params: float32 [2, 3158016], P(None, 'fsdp')
- new_first: float32 [2, 3158016], P(None, 'fsdp')
- new_second: float32 [2, 3158016], P(None, 'fsdp')
The draws below stay inside these ranges and needn't reach their ends.
Inputs may be any that keep to these rules, and one draw needn't show every extreme that they name: Each device holds counts images in its first slots; every device holds 1 or 0 images, some device holds 1 and some holds 0.
All inputs are finite; a program needn't handle non-finite values.
Results may differ from the reference program's by a relative error of at most 0.017.
Values may be sent and summed in bfloat16 or wider, within the bound.
No kernel may reach another device: no remote copies, remote signals or barrier semaphores. Data moves between devices by JAX's collectives and lax.ppermute only.
A program may use at most 192 MiB of HBM per device.

```python
import math
import jax
import jax.numpy as jnp
import numpy as np
from jax import lax

C = 512
HEADS = 16
FF = 2048
HEAD_DIM = 32
WIN = 7
SIDE = 14
SHIFT = 3
STEP = 3
IMG_DEV = 1
TABLE = 169
WTOK = 49
IMG_TOK = 196
SLOTS = 32
FLAT = 3158016


def draw_images(key, part):
    key_a, key_b, key_c = jax.random.split(key, 3)
    full_shape = (SLOTS, IMG_TOK, C)
    row_scale = 10.0 ** jax.random.uniform(key_b, (SLOTS, IMG_TOK, 1), minval=0.0, maxval=0.5)
    col_scale = 10.0 ** jax.random.uniform(key_c, (1, 1, C), minval=-0.5, maxval=0.5)
    base = jax.random.truncated_normal(key_a, -4.0, 4.0, full_shape)
    return (base * row_scale * col_scale).astype(jnp.float32)


def draw_cotangent(key, part):
    key_a, key_b = jax.random.split(key, 2)
    full_shape = (SLOTS, IMG_TOK, C)
    slot_scale = 3.0 ** (jnp.arange(SLOTS, dtype=jnp.float32) / max(SLOTS - 1, 1))
    row_scale = 10.0 ** jax.random.uniform(key_b, (SLOTS, IMG_TOK, 1), minval=0.0, maxval=0.5)
    base = jax.random.truncated_normal(key_a, -4.0, 4.0, full_shape)
    return (base * row_scale * slot_scale[:, None, None]).astype(jnp.float32)


def draw_counts(key, part):
    key_a, key_b = jax.random.split(key)
    devices_all = SLOTS // IMG_DEV
    lighter = (jax.random.randint(key_a, (devices_all,), 0, 3) == 0).astype(jnp.int32)
    values = IMG_DEV - lighter
    order = jax.random.permutation(key_b, devices_all)
    values = values.at[order[0]].set(IMG_DEV).at[order[1]].set(IMG_DEV - 1)
    return values.astype(jnp.int32)


def draw_params(key, part):
    key_a = jax.random.fold_in(key, 0)
    position = jnp.arange(FLAT)
    spread_all = jnp.full((FLAT,), 0.1, jnp.float32)
    center_all = jnp.zeros((FLAT,), jnp.float32)
    segments = ((3 * C * C, C ** (-0.5), 0.0), (C * C, 3.0 * C ** (-0.5), 0.0), (C * FF, C ** (-0.5), 0.0), (FF * C, FF ** (-0.5), 0.0), (TABLE * HEADS, 1.0, 0.0), (C, 0.25, 1.0), (C, 0.3, 0.0), (C, 0.3, 0.0), (C, 0.3, 0.0), (C, 0.3, 0.0), (C, 0.25, 1.0), (C, 0.3, 0.0), (C, 0.3, 0.0), (FF, 0.3, 0.0))
    start_at = 0
    for length, spread, middle in segments:
        inside = (position >= start_at) & (position < start_at + length)
        spread_all = jnp.where(inside, spread, spread_all)
        center_all = jnp.where(inside, middle, center_all)
        start_at += length
    noise = jax.random.truncated_normal(key_a, -3.0, 3.0, (2, FLAT))
    values = center_all + spread_all * noise
    return values.astype(jnp.float32)


def levels(own_key, extent, cuts, low, high):
    gain = 1.0
    for axis_at, parts in cuts:
        draws = jax.random.uniform(jax.random.fold_in(jax.random.fold_in(own_key, 6), axis_at), (parts,), jnp.float32, low / len(cuts), high / len(cuts))
        gain = gain * jnp.repeat(jnp.exp(draws), extent[axis_at] // parts).reshape((-1,) + (1,) * (len(extent) - 1 - axis_at))
    return gain


def scatter_about(stream_key, dims, deviation, most, cuts=(), kind=jnp.bfloat16):
    entries = jax.random.normal(stream_key, dims, jnp.float32) * deviation
    if len(cuts) > 0:
        entries = levels(stream_key, dims, cuts, -0.22, 0.18) * entries
    return jnp.clip(entries, min=-most, max=most).astype(kind)


def setup_inputs(seed: int = 0) -> dict:
    splits = jax.random.split(jax.random.key(seed), 7)
    images = draw_images(jax.random.fold_in(splits[6], 71), 0)
    counts = draw_counts(jax.random.fold_in(splits[6], 71), 0)
    cotangent = draw_cotangent(jax.random.fold_in(splits[6], 71), 0)
    params = draw_params(jax.random.fold_in(splits[6], 71), 0)
    first_moment = scatter_about(splits[4], (2, FLAT), 3.0, 12.0, ((1, 32),), jnp.float32)
    second_moment = jnp.clip(jnp.exp(math.log(100.0) - 4.6051702 * jax.random.uniform(splits[5], (2, FLAT), jnp.float32) ** levels(splits[5], (2, FLAT), ((1, 32),), -0.2, 0.2)), 1.0, 100.0)
    return {"images": images, "counts": counts, "cotangent": cotangent, "params": params, "first_moment": first_moment, "second_moment": second_moment}


EPS_NORM = 1e-05
LEARN_RATE = 0.02
WEIGHT_DECAY = 0.1
BETA_FIRST = 0.9
BETA_SECOND = 0.95
EPS_ADAM = 1e-08
MASKED = -1e+30

def entry_list():
    return (('w_qkv', (C, 3 * C)), ('w_out', (C, C)), ('w_fc1', (C, FF)), ('w_fc2', (FF, C)), ('table', (TABLE, HEADS)), ('vectors', (8, C)), ('b_fc1', (FF,)))

def unpack(flat_values):
    pieces = {}
    position = 0
    for entry_name, entry_shape in entry_list():
        length = math.prod(entry_shape)
        pieces[entry_name] = flat_values[position:position + length].reshape(entry_shape)
        position += length
    return pieces

def pack(pieces, total_length):
    parts_all = [pieces[entry_name].reshape(-1) for entry_name, entry_shape in entry_list()]
    used_length = sum((part.shape[0] for part in parts_all))
    parts_all.append(jnp.zeros((total_length - used_length,), jnp.float32))
    return jnp.concatenate(parts_all)

def offset_onehot():
    row_pos = np.arange(WTOK) // WIN
    col_pos = np.arange(WTOK) % WIN
    span_count = 2 * WIN - 1
    rel_index = (row_pos[:, None] - row_pos[None, :] + WIN - 1) * span_count + (col_pos[:, None] - col_pos[None, :] + WIN - 1)
    table_ids = np.arange(TABLE)
    return jnp.asarray(rel_index.reshape(-1)[:, None] == table_ids[None, :]).astype(jnp.float32)

def region_mask():
    coords = np.arange(SIDE)
    labels = (coords >= SIDE - WIN).astype(np.int64) + (coords >= SIDE - SHIFT).astype(np.int64)
    region = labels[:, None] * 3 + labels[None, :]
    grid_count = SIDE // WIN
    region = region.reshape(grid_count, WIN, grid_count, WIN).transpose(0, 2, 1, 3).reshape(grid_count * grid_count, WTOK)
    return jnp.asarray(region[:, :, None] == region[:, None, :])

def to_windows(tokens, shifted):
    count_img = tokens.shape[0]
    feature = tokens.shape[-1]
    grid_count = SIDE // WIN
    spatial = tokens.reshape(count_img, SIDE, SIDE, feature)
    if shifted:
        spatial = jnp.roll(spatial, (-SHIFT, -SHIFT), (1, 2))
    blocks = spatial.reshape(count_img, grid_count, WIN, grid_count, WIN, feature).transpose(0, 1, 3, 2, 4, 5)
    return blocks.reshape(count_img * grid_count * grid_count, WTOK, feature)

def from_windows(windows, shifted):
    grid_count = SIDE // WIN
    feature = windows.shape[-1]
    count_img = windows.shape[0] // (grid_count * grid_count)
    spatial = windows.reshape(count_img, grid_count, grid_count, WIN, WIN, feature).transpose(0, 1, 3, 2, 4, 5)
    spatial = spatial.reshape(count_img, SIDE, SIDE, feature)
    if shifted:
        spatial = jnp.roll(spatial, (SHIFT, SHIFT), (1, 2))
    return spatial.reshape(count_img, IMG_TOK, feature)

def norm_forward(stream, gain_row, shift_row):
    mean_row = lax.optimization_barrier(jnp.mean(stream, axis=-1, keepdims=True))
    centered = stream - mean_row
    inv_std = lax.rsqrt(lax.optimization_barrier(jnp.mean(centered * centered, axis=-1, keepdims=True)) + EPS_NORM)
    normed = centered * inv_std
    return (normed, inv_std, (normed * gain_row + shift_row).astype(jnp.bfloat16))

def norm_backward(grad_hidden, normed, inv_std, gain_row):
    d_normed = grad_hidden * gain_row
    grad_in = inv_std * (d_normed - lax.optimization_barrier(jnp.mean(d_normed, axis=-1, keepdims=True)) - normed * lax.optimization_barrier(jnp.mean(d_normed * normed, axis=-1, keepdims=True)))
    return (grad_in, lax.optimization_barrier(jnp.sum(grad_hidden * normed, axis=0)), lax.optimization_barrier(jnp.sum(grad_hidden, axis=0)))

def gelu_parts(pre_act):
    cdf_part = 0.5 * (1.0 + lax.erf(pre_act * 0.7071067811865476))
    slope_part = cdf_part + pre_act * jnp.exp(-0.5 * pre_act * pre_act) * 0.3989422804014327
    return (pre_act * cdf_part, slope_part)

def relative_bias(table_b):
    looked = jnp.dot(offset_onehot(), table_b.astype(jnp.float32), precision=lax.Precision.HIGHEST)
    return looked.reshape(WTOK, WTOK, HEADS).transpose(2, 0, 1)

def window_scores(query_b, key_b, bias_full, shifted):
    scores = jnp.einsum('nqhd,nkhd->nhqk', query_b.astype(jnp.float32), key_b.astype(jnp.float32)) + bias_full[None]
    if shifted:
        count_win = query_b.shape[0]
        region = jnp.tile(region_mask(), (count_win // region_mask().shape[0], 1, 1))[:, None]
        scores = jnp.where(region, scores, MASKED)
    return scores

def layer_forward(stream, weights, shifted):
    count_img = stream.shape[0]
    rows_all = count_img * IMG_TOK
    score_scale = HEAD_DIM ** (-0.5)
    vectors = weights['vectors'].astype(jnp.float32)
    stream_rows = stream.reshape(rows_all, C)
    normed_one, inv_one, hidden_one = norm_forward(stream_rows, vectors[0], vectors[1])
    windows_in = to_windows(hidden_one.reshape(count_img, IMG_TOK, C), shifted).reshape(rows_all, C)
    qkv_all = jnp.dot(windows_in, weights['w_qkv'], preferred_element_type=jnp.float32)
    head_shape = (-1, WTOK, HEADS, HEAD_DIM)
    query_b = ((qkv_all[:, :C] + vectors[2]) * score_scale).astype(jnp.bfloat16).reshape(head_shape)
    key_b = qkv_all[:, C:2 * C].astype(jnp.bfloat16).reshape(head_shape)
    value_b = (qkv_all[:, 2 * C:] + vectors[3]).astype(jnp.bfloat16).reshape(head_shape)
    bias_full = relative_bias(weights['table'])
    scores = window_scores(query_b, key_b, bias_full, shifted)
    row_max = lax.optimization_barrier(jnp.max(scores, axis=-1, keepdims=True))
    log_total = row_max + jnp.log(lax.optimization_barrier(jnp.sum(jnp.exp(scores - row_max), axis=-1, keepdims=True)))
    probs_b = jnp.exp(scores - log_total).astype(jnp.bfloat16)
    attended = jnp.einsum('nhqk,nkhd->nqhd', probs_b.astype(jnp.float32), value_b.astype(jnp.float32))
    attended = attended.astype(jnp.bfloat16).reshape(-1, WTOK, C)
    attended_tok = from_windows(attended, shifted).reshape(rows_all, C)
    projected = jnp.dot(attended_tok, weights['w_out'], preferred_element_type=jnp.float32) + vectors[4]
    mid_stream = stream_rows + projected
    normed_two, inv_two, hidden_two = norm_forward(mid_stream, vectors[5], vectors[6])
    pre_act = jnp.dot(hidden_two, weights['w_fc1'], preferred_element_type=jnp.float32) + weights['b_fc1'].astype(jnp.float32)
    act_f, gelu_slope = gelu_parts(pre_act)
    act_b = act_f.astype(jnp.bfloat16)
    result = mid_stream + jnp.dot(act_b, weights['w_fc2'], preferred_element_type=jnp.float32) + vectors[7]
    kept_values = (normed_one, inv_one, windows_in, query_b, key_b, value_b, bias_full, log_total, attended_tok, normed_two, inv_two, hidden_two, gelu_slope, act_b)
    return (result.reshape(count_img, IMG_TOK, C), kept_values)

def layer_backward(grad_out, kept_values, weights, shifted):
    normed_one, inv_one, windows_in, query_b, key_b, value_b, bias_full, log_total, attended_tok, normed_two, inv_two, hidden_two, gelu_slope, act_b = kept_values
    count_img = grad_out.shape[0]
    rows_all = count_img * IMG_TOK
    score_scale = HEAD_DIM ** (-0.5)
    vectors = weights['vectors'].astype(jnp.float32)
    grad_rows = grad_out.reshape(rows_all, C)
    grad_rows_b = grad_rows.astype(jnp.bfloat16)
    g_fc2 = jnp.dot(act_b.T, grad_rows_b, preferred_element_type=jnp.float32)
    d_pre = jnp.dot(grad_rows_b, weights['w_fc2'].T, preferred_element_type=jnp.float32) * gelu_slope
    d_pre_b = d_pre.astype(jnp.bfloat16)
    g_fc1 = jnp.dot(hidden_two.T, d_pre_b, preferred_element_type=jnp.float32)
    d_hidden_two = jnp.dot(d_pre_b, weights['w_fc1'].T, preferred_element_type=jnp.float32)
    d_norm_two, g_gain_two, g_shift_two = norm_backward(d_hidden_two, normed_two, inv_two, vectors[5])
    d_mid = grad_rows + d_norm_two
    d_mid_b = d_mid.astype(jnp.bfloat16)
    g_out = jnp.dot(attended_tok.T, d_mid_b, preferred_element_type=jnp.float32)
    d_att = jnp.dot(d_mid_b, weights['w_out'].T, preferred_element_type=jnp.float32).astype(jnp.bfloat16)
    d_att_win = to_windows(d_att.reshape(count_img, IMG_TOK, C), shifted).reshape(-1, WTOK, HEADS, HEAD_DIM)
    scores = window_scores(query_b, key_b, bias_full, shifted)
    attn_probs = jnp.exp(scores - log_total)
    probs_b = attn_probs.astype(jnp.bfloat16)
    d_probs = jnp.einsum('nqhd,nkhd->nhqk', d_att_win.astype(jnp.float32), value_b.astype(jnp.float32))
    d_value = jnp.einsum('nhqk,nqhd->nkhd', probs_b.astype(jnp.float32), d_att_win.astype(jnp.float32))
    d_scores = attn_probs * (d_probs - lax.optimization_barrier(jnp.sum(d_probs * attn_probs, axis=-1, keepdims=True)))
    d_scores_b = d_scores.astype(jnp.bfloat16)
    d_query = jnp.einsum('nhqk,nkhd->nqhd', d_scores_b.astype(jnp.float32), key_b.astype(jnp.float32)) * score_scale
    d_key = jnp.einsum('nhqk,nqhd->nkhd', d_scores_b.astype(jnp.float32), query_b.astype(jnp.float32))
    d_bias = lax.optimization_barrier(jnp.sum(d_scores, axis=0)).transpose(1, 2, 0).reshape(WTOK * WTOK, HEADS)
    g_table = jnp.dot(offset_onehot().T, d_bias, precision=lax.Precision.HIGHEST)
    d_query_rows = d_query.reshape(rows_all, C)
    d_value_rows = d_value.reshape(rows_all, C)
    d_qkv_b = jnp.concatenate([d_query_rows, d_key.reshape(rows_all, C), d_value_rows], axis=1).astype(jnp.bfloat16)
    g_qkv = jnp.dot(windows_in.T, d_qkv_b, preferred_element_type=jnp.float32)
    d_hidden_win = jnp.dot(d_qkv_b, weights['w_qkv'].T, preferred_element_type=jnp.float32)
    d_hidden_one = from_windows(d_hidden_win.reshape(-1, WTOK, C), shifted).reshape(rows_all, C)
    d_norm_one, g_gain_one, g_shift_one = norm_backward(d_hidden_one, normed_one, inv_one, vectors[0])
    grad_in = d_mid + d_norm_one
    g_vectors = jnp.stack([g_gain_one, g_shift_one, lax.optimization_barrier(jnp.sum(d_query_rows, axis=0)), lax.optimization_barrier(jnp.sum(d_value_rows, axis=0)), lax.optimization_barrier(jnp.sum(d_mid, axis=0)), g_gain_two, g_shift_two, lax.optimization_barrier(jnp.sum(grad_rows, axis=0))])
    grad_terms = {'w_qkv': g_qkv, 'w_out': g_out, 'w_fc1': g_fc1, 'w_fc2': g_fc2, 'table': g_table, 'vectors': g_vectors, 'b_fc1': lax.optimization_barrier(jnp.sum(d_pre, axis=0))}
    return (grad_in.reshape(count_img, IMG_TOK, C), grad_terms)

def adam_update(weights_now, grads_now, moment_one, moment_two):
    new_one = BETA_FIRST * moment_one + (1.0 - BETA_FIRST) * grads_now
    new_two = BETA_SECOND * moment_two + (1.0 - BETA_SECOND) * grads_now * grads_now
    corr_one = 1.0 - BETA_FIRST ** STEP
    corr_two = 1.0 - BETA_SECOND ** STEP
    update = new_one / corr_one / (jnp.sqrt(new_two / corr_two) + EPS_ADAM)
    return (weights_now - LEARN_RATE * (update + WEIGHT_DECAY * weights_now), new_one, new_two)

def reference(images, counts, cotangent, params, first_moment, second_moment):
    slot_ids = jnp.arange(SLOTS)
    slot_valid = (slot_ids % IMG_DEV < counts[slot_ids // IMG_DEV]).astype(jnp.float32)
    weights_one = unpack(params[0].astype(jnp.bfloat16))
    weights_two = unpack(params[1].astype(jnp.bfloat16))
    group_size = IMG_DEV * min(8, SLOTS // IMG_DEV)
    group_count = SLOTS // group_size

    def one_group(running, inputs):
        block_in, block_cot, block_valid = inputs
        mask_img = block_valid[:, None, None]
        stream_one, kept_one = layer_forward(block_in, weights_one, False)
        result, kept_two = layer_forward(stream_one, weights_two, True)
        grad_mid, terms_two = layer_backward(block_cot * mask_img, kept_two, weights_two, True)
        grad_first, terms_one = layer_backward(grad_mid, kept_one, weights_one, False)
        running = (jax.tree.map(jnp.add, running[0], terms_one), jax.tree.map(jnp.add, running[1], terms_two))
        return (running, (result * mask_img, grad_first * mask_img))
    zero_terms = {entry_name: jnp.zeros(entry_shape, jnp.float32) for entry_name, entry_shape in entry_list()}
    inputs = (images.reshape(group_count, group_size, IMG_TOK, C), cotangent.reshape(group_count, group_size, IMG_TOK, C), slot_valid.reshape(group_count, group_size))
    totals, (outputs, grads_in) = lax.scan(one_group, (zero_terms, zero_terms), inputs)
    param_grads = jnp.stack([pack(totals[0], FLAT), pack(totals[1], FLAT)])
    new_params, new_first, new_second = adam_update(params, param_grads, first_moment, second_moment)
    return (outputs.reshape(SLOTS, IMG_TOK, C), grads_in.reshape(SLOTS, IMG_TOK, C), param_grads, new_params, new_first, new_second)
```

```python
import functools
import math

import jax
import jax.numpy as jnp
import numpy as np
from jax import lax
from jax.experimental import pallas as pl
from jax.experimental.pallas import tpu as pltpu
from jax.sharding import Mesh
from jax.sharding import PartitionSpec as P

C = 512
HEADS = 16
FF = 2048
HEAD_DIM = 32
WIN = 7
SIDE = 14
SHIFT = 3
STEP = 3
TABLE = 169
WTOK = 49
IMG_TOK = 196

EPS_NORM = 1e-05
LEARN_RATE = 0.02
WEIGHT_DECAY = 0.1
BETA_FIRST = 0.9
BETA_SECOND = 0.95
EPS_ADAM = 1e-08
MASKED = -1e30

LANES = 128
NWIN = 4
WPAD = 64
ROWS = NWIN * WPAD
TPAD = 176
TOUT = 200

BASE_QKV, PITCH_QKV = 0, 12
BASE_OUT, PITCH_OUT = 6144, 4
BASE_FC1, PITCH_FC1 = 8192, 16
BASE_FC2, PITCH_FC2 = 16384, 4
BASE_TAIL = 24576
TAIL_VEC = 21
VEC_SKIP = 16
VEC_ROWS = 48

F32 = jnp.float32
BF16 = jnp.bfloat16


def round_up(value, unit):
    return (value + unit - 1) // unit * unit


def window_index(shifted):
    index = np.full((ROWS,), -1, np.int64)
    for wi in range(2):
        for wj in range(2):
            for ra in range(WIN):
                for ca in range(WIN):
                    i, j = wi * WIN + ra, wj * WIN + ca
                    if shifted:
                        i, j = (i + SHIFT) % SIDE, (j + SHIFT) % SIDE
                    index[(wi * 2 + wj) * WPAD + ra * WIN + ca] = i * SIDE + j
    return index


def order_matrices():
    first, second = window_index(False), window_index(True)
    take_first = np.zeros((ROWS, ROWS), np.float32)
    take_second = np.zeros((ROWS, ROWS), np.float32)
    for row in range(ROWS):
        if first[row] >= 0:
            take_first[row, first[row]] = 1.0
        if second[row] >= 0:
            take_second[row, second[row]] = 1.0
    return take_first, take_second


def key_masks():
    coords = np.arange(SIDE)
    labels = (coords >= SIDE - WIN).astype(np.int64) + (coords >= SIDE - SHIFT).astype(np.int64)
    region = labels[:, None] * 3 + labels[None, :]
    region = region.reshape(2, WIN, 2, WIN).transpose(0, 2, 1, 3).reshape(NWIN, WTOK)
    masks = np.zeros((2, NWIN, WPAD, WPAD), np.float32)
    masks[:, :, :, WTOK:] = MASKED
    masks[1, :, :WTOK, :WTOK] = np.where(region[:, :, None] == region[:, None, :], 0.0, MASKED)
    return np.concatenate([masks, masks], axis=-1)


def table_constants():
    offset = np.arange(TPAD)
    rows = (offset[:, None] // 8 == np.arange(24)[None, :]).astype(np.float32)
    lane = np.arange(LANES)
    lane_mask = (offset[:, None] % 8 == lane[None, :] // 16).astype(np.float32)
    order = np.concatenate([np.arange(0, HEADS, 2), np.arange(1, HEADS, 2)])
    heads = (lane[None, :] % 16 == order[:, None]).astype(np.float32)
    return rows, lane_mask, heads


def offset_lanes():
    lane = lax.broadcasted_iota(jnp.int32, (TPAD, WTOK, LANES), 2) % WPAD
    query = lax.broadcasted_iota(jnp.int32, (TPAD, WTOK, LANES), 1)
    want = lax.broadcasted_iota(jnp.int32, (TPAD, WTOK, LANES), 0)
    span = 2 * WIN - 1
    have = (query // WIN - lane // WIN + WIN - 1) * span + (query % WIN - lane % WIN + WIN - 1)
    hit = (have == want) & (lane < WTOK)
    return hit.astype(BF16).reshape(TPAD, WTOK * LANES)


def dot(a, b):
    return lax.dot_general(a, b, (((1,), (0,)), ((), ())), preferred_element_type=F32)


def dot_nt(a, b):
    return lax.dot_general(a, b, (((1,), (1,)), ((), ())), preferred_element_type=F32)


def dot_tn(a, b):
    return lax.dot_general(a, b, (((0,), (0,)), ((), ())), preferred_element_type=F32)


def select_rows(onehot, values):
    high = values.astype(BF16)
    rest = values - high.astype(F32)
    middle = rest.astype(BF16)
    low = (rest - middle.astype(F32)).astype(BF16)
    return dot(onehot, high) + dot(onehot, middle) + dot(onehot, low)


def flat_to_staging(flat_ref, block, staging, device_count, shard_rows):
    group = 8

    @pl.loop(0, device_count // group)
    def _(step):
        view = staging.at[pl.ds(pl.multiple_of(step * group * shard_rows, 8), group * shard_rows), :]
        for i in range(group):
            view[i * shard_rows : (i + 1) * shard_rows, :] = flat_ref[
                step * group + i, block, :shard_rows, :
            ].astype(F32)


def staging_to_flat(staging, flat_ref, device_count, shard_rows, padded_rows):
    group = 8

    @pl.loop(0, device_count // group)
    def _(step):
        view = staging.at[pl.ds(pl.multiple_of(step * group * shard_rows, 8), group * shard_rows), :]
        for i in range(group):
            flat_ref[step * group + i, :shard_rows, :] = view[
                i * shard_rows : (i + 1) * shard_rows, :
            ].astype(BF16)
            if padded_rows > shard_rows:
                flat_ref[step * group + i, shard_rows:, :] = jnp.zeros(
                    (padded_rows - shard_rows, LANES), BF16
                )


def unpack_matrix(staging, target, base, pitch, chunk):
    rows = target.shape[0]

    @pl.loop(0, rows // chunk)
    def _(step):
        start = pl.multiple_of(base + step * (chunk * pitch), 8)
        view = staging.at[pl.ds(start, chunk * pitch), :]
        row = pl.multiple_of(step * chunk, chunk)
        for j in range(pitch):
            target[pl.ds(row, chunk), j * LANES : (j + 1) * LANES] = view[
                pl.ds(j, chunk, stride=pitch), :
            ].astype(BF16)


def pack_matrix(staging, values, base, pitch, first_col):
    rows, cols = values.shape
    view = staging.at[pl.ds(base, rows * pitch), :]
    for j in range(cols // LANES):
        view[pl.ds(first_col + j, rows, stride=pitch), :] = values[:, j * LANES : (j + 1) * LANES]


def lane_ids(shape):
    return lax.broadcasted_iota(jnp.int32, shape, len(shape) - 1)


def unpack_tail(staging, shift_ref, tail_rows):
    tail = staging[BASE_TAIL : BASE_TAIL + 96, :]
    shift_ref[...] = pltpu.roll(tail, LANES - VEC_SKIP, 1)
    low = shift_ref[TAIL_VEC : TAIL_VEC + VEC_ROWS, :]
    high = shift_ref[TAIL_VEC + 1 : TAIL_VEC + 1 + VEC_ROWS, :]
    joined = jnp.where(lane_ids((VEC_ROWS, LANES)) < LANES - VEC_SKIP, low, high)
    vectors = [
        jnp.concatenate([joined[4 * v + i : 4 * v + i + 1, :] for i in range(4)], axis=1)
        for v in range(8)
    ]
    b_fc1 = jnp.concatenate([joined[32 + i : 33 + i, :] for i in range(16)], axis=1)
    return vectors, b_fc1


def build_bias(staging, rows_ref, lane_mask_ref, heads_ref, offsets_ref, bias_ref):
    block = staging[BASE_TAIL : BASE_TAIL + 24, :].astype(BF16)
    spread = dot(rows_ref[...], block) * lane_mask_ref[...].astype(F32)
    table = dot_nt(heads_ref[...], spread.astype(BF16)).astype(BF16)
    bias_ref[...] = jnp.zeros_like(bias_ref)
    even = lane_ids((8, LANES)) < WPAD
    for a in range(WTOK):
        both = dot(table, offsets_ref[:, a * LANES : (a + 1) * LANES])
        bias_ref[pl.ds(a, 8, stride=WPAD), :] = jnp.where(even, both[:8], both[8:])


def norm_rows(values):
    mean = jnp.mean(values, axis=-1, keepdims=True)
    centered = values - mean
    inv_std = lax.rsqrt(jnp.mean(centered * centered, axis=-1, keepdims=True) + EPS_NORM)
    return centered * inv_std, inv_std


def norm_grad(grad_hidden, normed, inv_std, gain_row):
    d_normed = grad_hidden * gain_row
    grad_in = inv_std * (
        d_normed
        - jnp.mean(d_normed, axis=-1, keepdims=True)
        - normed * jnp.mean(d_normed * normed, axis=-1, keepdims=True)
    )
    return (
        grad_in,
        jnp.sum(grad_hidden * normed, axis=0, keepdims=True),
        jnp.sum(grad_hidden, axis=0, keepdims=True),
    )


def erf(x):
    return lax.erf(x)


def pair_masks():
    lane = lane_ids((1, 256))
    pair = [(lane // 64 == h).astype(F32).astype(BF16) for h in range(4)]
    even = (lane % 64 < 32).astype(F32).astype(BF16)
    odd = (lane % 64 >= 32).astype(F32).astype(BF16)
    pair_f = [(lane // 64 == h).astype(F32) for h in range(4)]
    return pair, even, odd, pair_f


def stack_pairs(values, pair):
    return jnp.concatenate([values * pair[h] for h in range(4)], axis=0)


def stack_halves(values, even, odd):
    return jnp.concatenate([values * even, values * odd], axis=0)


def gather_pairs(values, pair_f):
    total = values[:WPAD] * pair_f[0]
    for h in range(1, 4):
        total = total + values[h * WPAD : (h + 1) * WPAD] * pair_f[h]
    return total


def half_sum(values, even_lane):
    left = jnp.sum(jnp.where(even_lane, values, 0.0), axis=-1, keepdims=True)
    right = jnp.sum(jnp.where(even_lane, 0.0, values), axis=-1, keepdims=True)
    return left, right


def block_forward(x, w, vec, b_fc1, bias_ref, mask_ref, kept):
    normed, inv_std = norm_rows(x)
    kept["n1"][...] = normed
    kept["r1"][...] = jnp.broadcast_to(inv_std, (ROWS, LANES))
    kept["h1"][...] = (normed * vec[0] + vec[1]).astype(BF16)
    scale = HEAD_DIM ** (-0.5)
    hidden = kept["h1"][...]
    kept["q"][...] = ((dot(hidden, w["qkv"][:, :C]) + vec[2]) * scale).astype(BF16)
    kept["k"][...] = dot(hidden, w["qkv"][:, C : 2 * C]).astype(BF16)
    kept["v"][...] = (dot(hidden, w["qkv"][:, 2 * C :]) + vec[3]).astype(BF16)

    @pl.loop(0, NWIN)
    def _(win):
        pair, even, odd, pair_f = pair_masks()
        even_lane = lane_ids((1, LANES)) < WPAD
        rows = pl.ds(pl.multiple_of(win * WPAD, WPAD), WPAD)
        mask = jnp.concatenate([mask_ref[win]] * 4, axis=0)
        for g in range(2):
            cols = slice(g * 256, (g + 1) * 256)
            query = stack_pairs(kept["q"][rows, cols], pair)
            key = stack_halves(kept["k"][rows, cols], even, odd)
            value = stack_halves(kept["v"][rows, cols], even, odd)
            scores = dot_nt(query, key) + bias_ref[cols, :] + mask
            left = jnp.max(jnp.where(even_lane, scores, -3e38), axis=-1, keepdims=True)
            right = jnp.max(jnp.where(even_lane, -3e38, scores), axis=-1, keepdims=True)
            expo = jnp.exp(scores - jnp.where(even_lane, left, right))
            left, right = half_sum(expo, even_lane)
            probs = expo * jnp.where(even_lane, 1.0 / left, 1.0 / right)
            kept["p"][win * 2 + g] = probs
            mixed = dot(probs.astype(BF16), value)
            kept["att"][rows, cols] = gather_pairs(mixed, pair_f).astype(BF16)

    mid = x + dot(kept["att"][...], w["out"][...]) + vec[4]
    normed, inv_std = norm_rows(mid)
    kept["n2"][...] = normed
    kept["r2"][...] = jnp.broadcast_to(inv_std, (ROWS, LANES))
    kept["h2"][...] = (normed * vec[5] + vec[6]).astype(BF16)
    result = mid + vec[7]
    for f in range(4):
        cols = slice(f * 512, (f + 1) * 512)
        pre = dot(kept["h2"][...], w["fc1"][:, cols]) + b_fc1[:, cols]
        cdf = 0.5 * (1.0 + erf(pre * 0.7071067811865476))
        slope = cdf + pre * jnp.exp(-0.5 * pre * pre) * 0.3989422804014327
        kept["slope"][:, cols] = slope.astype(kept["slope"].dtype)
        act = (pre * cdf).astype(BF16)
        kept["act"][:, cols] = act
        result = result + dot(act, w["fc2"][cols, :])
    return result


def block_backward(dout, w, gain_one, gain_two, kept, staging, consts, scratch, device_count, shard_rows):
    rows_ref, lane_mask_ref, heads_ref, offsets_ref = consts
    datt_ref, dqkv_ref, dbias_ref, spread_hi, spread_lo, vec_rows = scratch
    grads = [None] * 8
    dout_b = dout.astype(BF16)
    grads[7] = jnp.sum(dout, axis=0, keepdims=True)
    g_b1 = []
    d_hidden = None
    for f in range(4):
        cols = slice(f * 512, (f + 1) * 512)
        pack_matrix(staging, dot_tn(kept["act"][:, cols], dout_b), BASE_FC2 + f * 512 * PITCH_FC2, PITCH_FC2, 0)
        d_pre = dot_nt(dout_b, w["fc2"][cols, :]) * kept["slope"][:, cols].astype(F32)
        g_b1.append(jnp.sum(d_pre, axis=0, keepdims=True))
        d_pre_b = d_pre.astype(BF16)
        pack_matrix(staging, dot_tn(kept["h2"][...], d_pre_b), BASE_FC1, PITCH_FC1, f * 4)
        term = dot_nt(d_pre_b, w["fc1"][:, cols])
        d_hidden = term if d_hidden is None else d_hidden + term
    d_norm, grads[5], grads[6] = norm_grad(d_hidden, kept["n2"][...], kept["r2"][:, :1], gain_two)
    d_mid = dout + d_norm
    d_mid_b = d_mid.astype(BF16)
    grads[4] = jnp.sum(d_mid, axis=0, keepdims=True)
    pack_matrix(staging, dot_tn(kept["att"][...], d_mid_b), BASE_OUT, PITCH_OUT, 0)
    datt_ref[...] = dot_nt(d_mid_b, w["out"][...]).astype(BF16)
    dbias_ref[...] = jnp.zeros_like(dbias_ref)
    vec_rows[0:16, :] = jnp.zeros((16, C), F32)
    scale = HEAD_DIM ** (-0.5)

    @pl.loop(0, NWIN)
    def _(win):
        pair, even, odd, pair_f = pair_masks()
        even_lane = lane_ids((1, LANES)) < WPAD
        even_col = lane_ids((1, 256)) % 64 < 32
        rows = pl.ds(pl.multiple_of(win * WPAD, WPAD), WPAD)
        for g in range(2):
            cols = slice(g * 256, (g + 1) * 256)
            query = stack_pairs(kept["q"][rows, cols], pair)
            key = stack_halves(kept["k"][rows, cols], even, odd)
            value = stack_halves(kept["v"][rows, cols], even, odd)
            d_att = stack_pairs(datt_ref[rows, cols], pair)
            probs = kept["p"][win * 2 + g]
            d_probs = dot_nt(d_att, value)
            left, right = half_sum(d_probs * probs, even_lane)
            d_scores = probs * (d_probs - jnp.where(even_lane, left, right))
            dbias_ref[cols, :] += d_scores
            d_scores_b = d_scores.astype(BF16)
            d_query = gather_pairs(dot(d_scores_b, key), pair_f) * scale
            d_key = dot_tn(d_scores_b, query)
            d_value = dot_tn(probs.astype(BF16), d_att)
            d_key = jnp.where(even_col, d_key[:WPAD], d_key[WPAD:])
            d_value = jnp.where(even_col, d_value[:WPAD], d_value[WPAD:])
            vec_rows[0:1, cols] += jnp.sum(d_query, axis=0, keepdims=True)
            vec_rows[8:9, cols] += jnp.sum(d_value, axis=0, keepdims=True)
            dqkv_ref[rows, cols] = d_query.astype(BF16)
            dqkv_ref[rows, C + g * 256 : C + (g + 1) * 256] = d_key.astype(BF16)
            dqkv_ref[rows, 2 * C + g * 256 : 2 * C + (g + 1) * 256] = d_value.astype(BF16)

    grads[2] = vec_rows[0:1, :]
    grads[3] = vec_rows[8:9, :]
    d_hidden = None
    for f in range(3):
        cols = slice(f * 512, (f + 1) * 512)
        pack_matrix(staging, dot_tn(kept["h1"][...], dqkv_ref[:, cols]), BASE_QKV, PITCH_QKV, f * 4)
        term = dot_nt(dqkv_ref[:, cols], w["qkv"][:, cols])
        d_hidden = term if d_hidden is None else d_hidden + term
    d_norm, grads[0], grads[1] = norm_grad(d_hidden, kept["n1"][...], kept["r1"][:, :1], gain_one)
    d_in = d_mid + d_norm

    even = lane_ids((8, LANES)) < WPAD
    for a in range(WTOK):
        part = dbias_ref[pl.ds(a, 8, stride=WPAD), :]
        part = jnp.concatenate([jnp.where(even, part, 0.0), jnp.where(even, 0.0, part)], axis=0)
        high = part.astype(BF16)
        spread_hi[:, a * LANES : (a + 1) * LANES] = high
        spread_lo[:, a * LANES : (a + 1) * LANES] = (part - high.astype(F32)).astype(BF16)
    g_table = dot_nt(offsets_ref[...], spread_hi[...]) + dot_nt(offsets_ref[...], spread_lo[...])
    g_lanes = dot(g_table.astype(BF16), heads_ref[...]) * lane_mask_ref[...].astype(F32)
    g_rows = dot_tn(rows_ref[...], g_lanes.astype(BF16))
    tail_rows = device_count * shard_rows - BASE_TAIL
    staging[BASE_TAIL : BASE_TAIL + tail_rows, :] = jnp.zeros((tail_rows, LANES), F32)
    staging[BASE_TAIL : BASE_TAIL + 24, :] = g_rows
    lines = []
    for v in range(8):
        lines += [grads[v][:, i * LANES : (i + 1) * LANES] for i in range(4)]
    for part in g_b1:
        lines += [part[:, i * LANES : (i + 1) * LANES] for i in range(4)]
    rolled = pltpu.roll(jnp.concatenate(lines, axis=0), VEC_SKIP, 1)
    first = lane_ids((VEC_ROWS, LANES)) < VEC_SKIP
    low = BASE_TAIL + TAIL_VEC
    staging[low : low + VEC_ROWS, :] += jnp.where(first, 0.0, rolled)
    staging[low + 1 : low + 1 + VEC_ROWS, :] += jnp.where(first, rolled, 0.0)
    return d_in


KEPT = {
    "n1": ((ROWS, C), F32),
    "r1": ((ROWS, LANES), F32),
    "h1": ((ROWS, C), BF16),
    "q": ((ROWS, C), BF16),
    "k": ((ROWS, C), BF16),
    "v": ((ROWS, C), BF16),
    "p": ((2 * NWIN, 256, LANES), F32),
    "att": ((ROWS, C), BF16),
    "n2": ((ROWS, C), F32),
    "r2": ((ROWS, LANES), F32),
    "h2": ((ROWS, C), BF16),
    "slope": ((ROWS, FF), F32),
    "act": ((ROWS, FF), BF16),
}
WEIGHTS = {
    "qkv": ((C, 3 * C), BF16),
    "out": ((C, C), BF16),
    "fc1": ((C, FF), BF16),
    "fc2": ((FF, C), BF16),
}
BACK_SCRATCH = [
    pltpu.VMEM((ROWS, C), BF16),
    pltpu.VMEM((ROWS, 3 * C), BF16),
    pltpu.VMEM((512, LANES), F32),
    pltpu.VMEM((16, WTOK * LANES), BF16),
    pltpu.VMEM((16, WTOK * LANES), BF16),
    pltpu.VMEM((16, C), F32),
]


def unpack_weights(flat_ref, block, staging, w, device_count, shard_rows):
    flat_to_staging(flat_ref, block, staging, device_count, shard_rows)
    unpack_matrix(staging, w["qkv"], BASE_QKV, PITCH_QKV, 128)
    unpack_matrix(staging, w["out"], BASE_OUT, PITCH_OUT, 128)
    unpack_matrix(staging, w["fc1"], BASE_FC1, PITCH_FC1, 128)
    unpack_matrix(staging, w["fc2"], BASE_FC2, PITCH_FC2, 256)


def first_kernel(sizes, *refs):
    device_count, shard_rows, padded_rows = sizes
    flat, images, order, mask, rows_c, lane_c, heads_c, offsets = refs[:8]
    names = list(KEPT) + list(WEIGHTS)
    stream, vec_out, *outs = refs[8 : 10 + len(names)]
    staging, shift, bias = refs[10 + len(names) :]
    kept = dict(zip(names, outs))
    unpack_weights(flat, 0, staging, kept, device_count, shard_rows)
    vec, b_fc1 = unpack_tail(staging, shift, None)
    vec_out[...] = jnp.concatenate(vec, axis=0)
    build_bias(staging, rows_c, lane_c, heads_c, offsets, bias)
    x = select_rows(order[...], images[...])
    stream[...] = block_forward(x, kept, vec, b_fc1, bias, mask, kept)


def second_kernel(sizes, *refs):
    device_count, shard_rows, padded_rows = sizes
    valid, flat, stream, cotangent, order, between, mask, rows_c, lane_c, heads_c, offsets = refs[:11]
    block_out, d_stream, grads = refs[11:14]
    names = list(KEPT) + list(WEIGHTS)
    kept = dict(zip(names, refs[14 : 14 + len(names)]))
    staging, shift, bias, *scratch = refs[14 + len(names) :]
    unpack_weights(flat, 0, staging, kept, device_count, shard_rows)
    vec, b_fc1 = unpack_tail(staging, shift, None)
    build_bias(staging, rows_c, lane_c, heads_c, offsets, bias)
    factor = (valid[0] > 0).astype(F32)
    x = select_rows(between[...], stream[...])
    result = block_forward(x, kept, vec, b_fc1, bias, mask, kept)
    back = order[...].T
    block_out[...] = select_rows(back, result)[:IMG_TOK] * factor
    dout = select_rows(order[...], cotangent[...]) * factor
    d_in = block_backward(
        dout, kept, vec[0], vec[5], kept, staging, (rows_c, lane_c, heads_c, offsets), scratch,
        device_count, shard_rows,
    )
    d_stream[...] = select_rows(between[...].T, d_in)
    staging_to_flat(staging, grads, device_count, shard_rows, padded_rows)


def third_kernel(sizes, *refs):
    device_count, shard_rows, padded_rows = sizes
    valid, d_stream, vec, order, rows_c, lane_c, heads_c, offsets = refs[:8]
    names = list(KEPT) + list(WEIGHTS)
    kept = dict(zip(names, refs[8 : 8 + len(names)]))
    input_grad, grads = refs[8 + len(names) : 10 + len(names)]
    staging, *scratch = refs[10 + len(names) :]
    factor = (valid[0] > 0).astype(F32)
    d_in = block_backward(
        d_stream[...], kept, vec[0:1, :], vec[5:6, :], kept, staging,
        (rows_c, lane_c, heads_c, offsets), scratch, device_count, shard_rows,
    )
    input_grad[...] = select_rows(order[...].T, d_in)[:IMG_TOK] * factor
    staging_to_flat(staging, grads, device_count, shard_rows, padded_rows)


VMEM_SPEC = pl.BlockSpec(memory_space=pltpu.VMEM)
SMEM_SPEC = pl.BlockSpec(memory_space=pltpu.SMEM)
PARAMS = pltpu.CompilerParams(vmem_limit_bytes=60 * 1024 * 1024)


def shapes_of(table):
    return [jax.ShapeDtypeStruct(shape, kind) for shape, kind in table.values()]


def scratch_of(table):
    return [pltpu.VMEM(shape, kind) for shape, kind in table.values()]


def axes_of(mesh):
    devices = list(mesh.devices.flat)
    coords = np.array([tuple(d.coords) + (d.core_on_chip,) for d in devices])
    extent = coords.max(axis=0) - coords.min(axis=0) + 1
    return int(extent[2]), int(extent[1]), int(extent[0]), int(extent[3])


def flip(values, axis):
    return lax.ppermute(values, axis, [(0, 1), (1, 0)])


def pick(values, dim, index):
    return lax.dynamic_index_in_dim(values, index, axis=dim, keepdims=False)


def reduce_rows(grads, sizes):
    names = ("z", "y", "x", "c")
    parts = [g.reshape(tuple(sizes) + g.shape[1:]) for g in grads]
    def halve(values, dim, name, size, bit):
        place = lax.axis_index(name)
        step = 1 << bit
        low = (place // step) % 2
        span = values.shape[dim]
        shaped = values.reshape(values.shape[:dim] + (span // 2, 2) + values.shape[dim + 1 :])
        sent = pick(shaped, dim + 1, 1 - low)
        pairs = [(i, i ^ step) for i in range(size)]
        return pick(shaped, dim + 1, low) + lax.ppermute(sent, name, pairs)

    def along(values, dim, name, size):
        bit = 0
        while (1 << bit) < size:
            values = halve(values, dim, name, size, bit)
            bit += 1
        return values

    z, y, x, c = sizes
    parts = [along(p, 3, "c", c) for p in parts]
    rows = parts[0].shape[4]
    cut = rows // 2 // 16 * 16
    first = [p[..., :cut, :] for p in parts]
    second = [p[..., cut:, :] for p in parts]
    first = [along(p, 2, "x", x) for p in first]
    second = [along(p, 1, "y", y) for p in second]
    first = [along(p, 1, "y", y) for p in first]
    second = [along(p, 2, "x", x) for p in second]
    parts = [jnp.concatenate([a, b], axis=4) for a, b in zip(first, second)]
    parts = [along(p, 0, "z", z) for p in parts]
    return [p.reshape(p.shape[4:]) for p in parts]


def adam_update(weights_now, grads_now, moment_one, moment_two):
    new_one = BETA_FIRST * moment_one + (1.0 - BETA_FIRST) * grads_now
    new_two = BETA_SECOND * moment_two + (1.0 - BETA_SECOND) * grads_now * grads_now
    corr_one = 1.0 - BETA_FIRST**STEP
    corr_two = 1.0 - BETA_SECOND**STEP
    update = new_one / corr_one / (jnp.sqrt(new_two / corr_two) + EPS_ADAM)
    return (weights_now - LEARN_RATE * (update + WEIGHT_DECAY * weights_now), new_one, new_two)


def local(sizes, images, counts, cotangent, params, first_moment, second_moment):
    device_count = math.prod(sizes)
    shard_len = params.shape[1]
    shard_rows = shard_len // LANES
    padded_rows = round_up(shard_rows, 16)
    dims = (device_count, shard_rows, padded_rows)
    flat_rows = device_count * shard_rows

    take_first, take_second = order_matrices()
    order_first = jnp.asarray(take_first[:, :], BF16)
    order_second = jnp.asarray(take_second, BF16)
    between = jnp.asarray(take_second @ take_first.T, BF16)
    masks = key_masks()
    mask_first, mask_second = jnp.asarray(masks[0]), jnp.asarray(masks[1])
    consts = [jnp.asarray(a, BF16) for a in table_constants()] + [offset_lanes()]

    shard = params.astype(BF16).reshape(2, shard_rows, LANES)
    shard = jnp.pad(shard, ((0, 0), (0, padded_rows - shard_rows), (0, 0)))
    axes = ("z", "y", "x", "c")
    flat_one = lax.all_gather(shard[0:1], axes, axis=0, tiled=False)
    flat_two = lax.all_gather(shard[1:2], axes, axis=0, tiled=False)

    pad_tokens = ((0, ROWS - IMG_TOK), (0, 0))
    image_rows = jnp.pad(images.reshape(IMG_TOK, C), pad_tokens)
    cot_rows = jnp.pad(cotangent.reshape(IMG_TOK, C), pad_tokens)

    grad_shape = jax.ShapeDtypeStruct((device_count, padded_rows, LANES), BF16)
    names = len(KEPT) + len(WEIGHTS)
    staging = pltpu.VMEM((flat_rows, LANES), F32)
    common = [staging, pltpu.VMEM((96, LANES), F32), pltpu.VMEM((512, LANES), F32)]
    stream, vec, *kept = pl.pallas_call(
        functools.partial(first_kernel, dims),
        out_shape=[
            jax.ShapeDtypeStruct((ROWS, C), F32),
            jax.ShapeDtypeStruct((8, C), F32),
            *shapes_of(KEPT),
            *shapes_of(WEIGHTS),
        ],
        in_specs=[VMEM_SPEC] * 8,
        out_specs=[VMEM_SPEC] * (2 + names),
        scratch_shapes=common,
        compiler_params=PARAMS,
        name="first",
    )(flat_one, image_rows, order_first, mask_first, *consts)

    block_out, d_stream, grads_two = pl.pallas_call(
        functools.partial(second_kernel, dims),
        out_shape=[
            jax.ShapeDtypeStruct((IMG_TOK, C), F32),
            jax.ShapeDtypeStruct((ROWS, C), F32),
            grad_shape,
        ],
        in_specs=[SMEM_SPEC] + [VMEM_SPEC] * 10,
        out_specs=[VMEM_SPEC] * 3,
        scratch_shapes=scratch_of(KEPT) + scratch_of(WEIGHTS) + common + BACK_SCRATCH,
        compiler_params=PARAMS,
        name="second",
    )(counts, flat_two, stream, cot_rows, order_second, between, mask_second, *consts)

    input_grad, grads_one = pl.pallas_call(
        functools.partial(third_kernel, dims),
        out_shape=[jax.ShapeDtypeStruct((IMG_TOK, C), F32), grad_shape],
        in_specs=[SMEM_SPEC] + [VMEM_SPEC] * (7 + names),
        out_specs=[VMEM_SPEC] * 2,
        scratch_shapes=[staging] + BACK_SCRATCH,
        compiler_params=PARAMS,
        name="third",
    )(counts, d_stream, vec, order_first, *consts, *kept)

    (sum_two,) = reduce_rows([grads_two], sizes)
    (sum_one,) = reduce_rows([grads_one], sizes)
    param_grads = jnp.stack([sum_one[:shard_rows], sum_two[:shard_rows]]).astype(F32)
    param_grads = param_grads.reshape(2, shard_len)
    new_params, new_first, new_second = adam_update(params, param_grads, first_moment, second_moment)
    return (
        block_out.reshape(1, IMG_TOK, C),
        input_grad.reshape(1, IMG_TOK, C),
        param_grads,
        new_params,
        new_first,
        new_second,
    )


def solution(mesh):
    sizes = axes_of(mesh)
    axes = ("z", "y", "x", "c")
    fine = Mesh(mesh.devices.reshape(sizes), axes)
    return jax.shard_map(
        functools.partial(local, sizes),
        mesh=fine,
        in_specs=(
            P(axes, None, None),
            P(axes),
            P(axes, None, None),
            P(None, axes),
            P(None, axes),
            P(None, axes),
        ),
        out_specs=(
            P(axes, None, None),
            P(axes, None, None),
            P(None, axes),
            P(None, axes),
            P(None, axes),
            P(None, axes),
        ),
        check_vma=False,
    )
```

```python
import functools
import math

import jax
import jax.numpy as jnp
import numpy as np
from jax import lax
from jax.experimental import pallas as pl
from jax.experimental.pallas import tpu as pltpu
from jax.sharding import Mesh
from jax.sharding import PartitionSpec as P

C = 512
HEADS = 16
FF = 2048
HEAD_DIM = 32
WIN = 7
SIDE = 14
SHIFT = 3
STEP = 3
TABLE = 169
WTOK = 49
IMG_TOK = 196

EPS_NORM = 1e-05
LEARN_RATE = 0.02
WEIGHT_DECAY = 0.1
BETA_FIRST = 0.9
BETA_SECOND = 0.95
EPS_ADAM = 1e-08
MASKED = -1e30

LANES = 128
NWIN = 4
WPAD = 64
ROWS = NWIN * WPAD
TPAD = 176
TOUT = 200

BASE_QKV, PITCH_QKV = 0, 12
BASE_OUT, PITCH_OUT = 6144, 4
BASE_FC1, PITCH_FC1 = 8192, 16
BASE_FC2, PITCH_FC2 = 16384, 4
BASE_TAIL = 24576
TAIL_VEC = 21
VEC_SKIP = 16
VEC_ROWS = 48

F32 = jnp.float32
BF16 = jnp.bfloat16


def round_up(value, unit):
    return (value + unit - 1) // unit * unit


def window_index(shifted):
    index = np.full((ROWS,), -1, np.int64)
    for wi in range(2):
        for wj in range(2):
            for ra in range(WIN):
                for ca in range(WIN):
                    i, j = wi * WIN + ra, wj * WIN + ca
                    if shifted:
                        i, j = (i + SHIFT) % SIDE, (j + SHIFT) % SIDE
                    index[(wi * 2 + wj) * WPAD + ra * WIN + ca] = i * SIDE + j
    return index


def order_matrices():
    first, second = window_index(False), window_index(True)
    take_first = np.zeros((ROWS, ROWS), np.float32)
    take_second = np.zeros((ROWS, ROWS), np.float32)
    for row in range(ROWS):
        if first[row] >= 0:
            take_first[row, first[row]] = 1.0
        if second[row] >= 0:
            take_second[row, second[row]] = 1.0
    return take_first, take_second


def key_masks():
    coords = np.arange(SIDE)
    labels = (coords >= SIDE - WIN).astype(np.int64) + (coords >= SIDE - SHIFT).astype(np.int64)
    region = labels[:, None] * 3 + labels[None, :]
    region = region.reshape(2, WIN, 2, WIN).transpose(0, 2, 1, 3).reshape(NWIN, WTOK)
    masks = np.zeros((2, NWIN, WPAD, WPAD), np.float32)
    masks[:, :, :, WTOK:] = MASKED
    masks[1, :, :WTOK, :WTOK] = np.where(region[:, :, None] == region[:, None, :], 0.0, MASKED)
    return np.concatenate([masks, masks], axis=-1)


def table_constants():
    offset = np.arange(TPAD)
    rows = (offset[:, None] // 8 == np.arange(24)[None, :]).astype(np.float32)
    lane = np.arange(LANES)
    lane_mask = (offset[:, None] % 8 == lane[None, :] // 16).astype(np.float32)
    order = np.concatenate([np.arange(0, HEADS, 2), np.arange(1, HEADS, 2)])
    heads = (lane[None, :] % 16 == order[:, None]).astype(np.float32)
    return rows, lane_mask, heads


def offset_lanes():
    lane = lax.broadcasted_iota(jnp.int32, (TPAD, WTOK, LANES), 2) % WPAD
    query = lax.broadcasted_iota(jnp.int32, (TPAD, WTOK, LANES), 1)
    want = lax.broadcasted_iota(jnp.int32, (TPAD, WTOK, LANES), 0)
    span = 2 * WIN - 1
    have = (query // WIN - lane // WIN + WIN - 1) * span + (query % WIN - lane % WIN + WIN - 1)
    hit = (have == want) & (lane < WTOK)
    return hit.astype(BF16).reshape(TPAD, WTOK * LANES)


def dot(a, b):
    return lax.dot_general(a, b, (((1,), (0,)), ((), ())), preferred_element_type=F32)


def dot_nt(a, b):
    return lax.dot_general(a, b, (((1,), (1,)), ((), ())), preferred_element_type=F32)


def dot_tn(a, b):
    return lax.dot_general(a, b, (((0,), (0,)), ((), ())), preferred_element_type=F32)


def select_rows(onehot, values):
    high = values.astype(BF16)
    rest = values - high.astype(F32)
    middle = rest.astype(BF16)
    low = (rest - middle.astype(F32)).astype(BF16)
    return dot(onehot, high) + dot(onehot, middle) + dot(onehot, low)


def fetch_pieces(pieces, buffer, sems, sizes, cut):
    z, y, x, _ = sizes
    view = buffer.reshape((z, y, x, 2) + buffer.shape[1:])
    copies = []
    at = 0
    for core in range(2):
        for part in range(2):
            rows = slice(0, cut) if part == 0 else slice(cut, buffer.shape[1])
            for late in range(2):
                piece = pieces[at]
                at += 1
                for i in range(piece.shape[1]):
                    for j in range(piece.shape[2]):
                        yy, xx = (i + late * piece.shape[1], j) if part == 0 else (i, j + late * piece.shape[2])
                        copies.append(
                            pltpu.make_async_copy(
                                piece.at[:, i, j], view.at[:, yy, xx, core, rows, :], sems.at[len(copies)]
                            )
                        )
    for copy in copies:
        copy.start()
    for copy in copies:
        copy.wait()


def flat_to_staging(buffer, staging, place, device_count, shard_rows):
    group = 8

    @pl.loop(0, device_count // group)
    def _(step):
        view = staging.at[pl.ds(pl.multiple_of(step * group * shard_rows, 8), group * shard_rows), :]
        for i in range(group):
            slot = lax.bitwise_xor(step * group + i, place)
            view[i * shard_rows : (i + 1) * shard_rows, :] = buffer[slot, :shard_rows, :].astype(F32)


def staging_to_flat(staging, keep_ref, send_ref, place, device_count, shard_rows, padded_rows):
    @pl.loop(0, device_count // 2)
    def _(pair):
        for core, target in enumerate((keep_ref, send_ref)):
            owner = lax.bitwise_xor(pair * 2 + core, place)
            target[pair, :shard_rows, :] = staging[pl.ds(owner * shard_rows, shard_rows), :].astype(BF16)
            if padded_rows > shard_rows:
                target[pair, shard_rows:, :] = jnp.zeros((padded_rows - shard_rows, LANES), BF16)


def unpack_matrix(staging, target, base, pitch, chunk):
    rows = target.shape[0]

    @pl.loop(0, rows // chunk)
    def _(step):
        start = pl.multiple_of(base + step * (chunk * pitch), 8)
        view = staging.at[pl.ds(start, chunk * pitch), :]
        row = pl.multiple_of(step * chunk, chunk)
        for j in range(pitch):
            target[pl.ds(row, chunk), j * LANES : (j + 1) * LANES] = view[
                pl.ds(j, chunk, stride=pitch), :
            ].astype(BF16)


def pack_matrix(staging, values, base, pitch, first_col):
    rows, cols = values.shape
    view = staging.at[pl.ds(base, rows * pitch), :]
    for j in range(cols // LANES):
        view[pl.ds(first_col + j, rows, stride=pitch), :] = values[:, j * LANES : (j + 1) * LANES]


def lane_ids(shape):
    return lax.broadcasted_iota(jnp.int32, shape, len(shape) - 1)


def unpack_tail(staging, shift_ref, tail_rows):
    tail = staging[BASE_TAIL : BASE_TAIL + 96, :]
    shift_ref[...] = pltpu.roll(tail, LANES - VEC_SKIP, 1)
    low = shift_ref[TAIL_VEC : TAIL_VEC + VEC_ROWS, :]
    high = shift_ref[TAIL_VEC + 1 : TAIL_VEC + 1 + VEC_ROWS, :]
    joined = jnp.where(lane_ids((VEC_ROWS, LANES)) < LANES - VEC_SKIP, low, high)
    vectors = [
        jnp.concatenate([joined[4 * v + i : 4 * v + i + 1, :] for i in range(4)], axis=1)
        for v in range(8)
    ]
    b_fc1 = jnp.concatenate([joined[32 + i : 33 + i, :] for i in range(16)], axis=1)
    return vectors, b_fc1


def build_bias(staging, rows_ref, lane_mask_ref, heads_ref, offsets_ref, bias_ref):
    block = staging[BASE_TAIL : BASE_TAIL + 24, :].astype(BF16)
    spread = dot(rows_ref[...], block) * lane_mask_ref[...].astype(F32)
    table = dot_nt(heads_ref[...], spread.astype(BF16)).astype(BF16)
    bias_ref[...] = jnp.zeros_like(bias_ref)
    even = lane_ids((8, LANES)) < WPAD
    for a in range(WTOK):
        both = dot(table, offsets_ref[:, a * LANES : (a + 1) * LANES])
        bias_ref[pl.ds(a, 8, stride=WPAD), :] = jnp.where(even, both[:8], both[8:])


def norm_rows(values):
    mean = jnp.mean(values, axis=-1, keepdims=True)
    centered = values - mean
    inv_std = lax.rsqrt(jnp.mean(centered * centered, axis=-1, keepdims=True) + EPS_NORM)
    return centered * inv_std, inv_std


def norm_grad(grad_hidden, normed, inv_std, gain_row):
    d_normed = grad_hidden * gain_row
    grad_in = inv_std * (
        d_normed
        - jnp.mean(d_normed, axis=-1, keepdims=True)
        - normed * jnp.mean(d_normed * normed, axis=-1, keepdims=True)
    )
    return (
        grad_in,
        jnp.sum(grad_hidden * normed, axis=0, keepdims=True),
        jnp.sum(grad_hidden, axis=0, keepdims=True),
    )


def erf(x):
    return lax.erf(x)


def pair_masks():
    lane = lane_ids((1, 256))
    pair = [(lane // 64 == h).astype(F32).astype(BF16) for h in range(4)]
    even = (lane % 64 < 32).astype(F32).astype(BF16)
    odd = (lane % 64 >= 32).astype(F32).astype(BF16)
    pair_f = [(lane // 64 == h).astype(F32) for h in range(4)]
    return pair, even, odd, pair_f


def stack_pairs(values, pair):
    return jnp.concatenate([values * pair[h] for h in range(4)], axis=0)


def stack_halves(values, even, odd):
    return jnp.concatenate([values * even, values * odd], axis=0)


def gather_pairs(values, pair_f):
    total = values[:WPAD] * pair_f[0]
    for h in range(1, 4):
        total = total + values[h * WPAD : (h + 1) * WPAD] * pair_f[h]
    return total


def half_sum(values, even_lane):
    left = jnp.sum(jnp.where(even_lane, values, 0.0), axis=-1, keepdims=True)
    right = jnp.sum(jnp.where(even_lane, 0.0, values), axis=-1, keepdims=True)
    return left, right


def block_forward(x, w, vec, b_fc1, bias_ref, mask_ref, kept):
    normed, inv_std = norm_rows(x)
    kept["n1"][...] = normed
    kept["r1"][...] = jnp.broadcast_to(inv_std, (ROWS, LANES))
    kept["h1"][...] = (normed * vec[0] + vec[1]).astype(BF16)
    scale = HEAD_DIM ** (-0.5)
    hidden = kept["h1"][...]
    kept["q"][...] = ((dot(hidden, w["qkv"][:, :C]) + vec[2]) * scale).astype(BF16)
    kept["k"][...] = dot(hidden, w["qkv"][:, C : 2 * C]).astype(BF16)
    kept["v"][...] = (dot(hidden, w["qkv"][:, 2 * C :]) + vec[3]).astype(BF16)

    @pl.loop(0, NWIN)
    def _(win):
        pair, even, odd, pair_f = pair_masks()
        even_lane = lane_ids((1, LANES)) < WPAD
        rows = pl.ds(pl.multiple_of(win * WPAD, WPAD), WPAD)
        mask = jnp.concatenate([mask_ref[win]] * 4, axis=0)
        for g in range(2):
            cols = slice(g * 256, (g + 1) * 256)
            query = stack_pairs(kept["q"][rows, cols], pair)
            key = stack_halves(kept["k"][rows, cols], even, odd)
            value = stack_halves(kept["v"][rows, cols], even, odd)
            scores = dot_nt(query, key) + bias_ref[cols, :] + mask
            left = jnp.max(jnp.where(even_lane, scores, -3e38), axis=-1, keepdims=True)
            right = jnp.max(jnp.where(even_lane, -3e38, scores), axis=-1, keepdims=True)
            expo = jnp.exp(scores - jnp.where(even_lane, left, right))
            left, right = half_sum(expo, even_lane)
            probs = expo * jnp.where(even_lane, 1.0 / left, 1.0 / right)
            kept["p"][win * 2 + g] = probs
            mixed = dot(probs.astype(BF16), value)
            kept["att"][rows, cols] = gather_pairs(mixed, pair_f).astype(BF16)

    mid = x + dot(kept["att"][...], w["out"][...]) + vec[4]
    normed, inv_std = norm_rows(mid)
    kept["n2"][...] = normed
    kept["r2"][...] = jnp.broadcast_to(inv_std, (ROWS, LANES))
    kept["h2"][...] = (normed * vec[5] + vec[6]).astype(BF16)
    result = mid + vec[7]
    for f in range(4):
        cols = slice(f * 512, (f + 1) * 512)
        pre = dot(kept["h2"][...], w["fc1"][:, cols]) + b_fc1[:, cols]
        cdf = 0.5 * (1.0 + erf(pre * 0.7071067811865476))
        slope = cdf + pre * jnp.exp(-0.5 * pre * pre) * 0.3989422804014327
        kept["slope"][:, cols] = slope.astype(kept["slope"].dtype)
        act = (pre * cdf).astype(BF16)
        kept["act"][:, cols] = act
        result = result + dot(act, w["fc2"][cols, :])
    return result


def block_backward(dout, w, gain_one, gain_two, kept, staging, consts, scratch, device_count, shard_rows):
    rows_ref, lane_mask_ref, heads_ref, offsets_ref = consts
    datt_ref, dqkv_ref, dbias_ref, spread_hi, spread_lo, vec_rows = scratch
    grads = [None] * 8
    dout_b = dout.astype(BF16)
    grads[7] = jnp.sum(dout, axis=0, keepdims=True)
    g_b1 = []
    d_hidden = None
    for f in range(4):
        cols = slice(f * 512, (f + 1) * 512)
        pack_matrix(staging, dot_tn(kept["act"][:, cols], dout_b), BASE_FC2 + f * 512 * PITCH_FC2, PITCH_FC2, 0)
        d_pre = dot_nt(dout_b, w["fc2"][cols, :]) * kept["slope"][:, cols].astype(F32)
        g_b1.append(jnp.sum(d_pre, axis=0, keepdims=True))
        d_pre_b = d_pre.astype(BF16)
        pack_matrix(staging, dot_tn(kept["h2"][...], d_pre_b), BASE_FC1, PITCH_FC1, f * 4)
        term = dot_nt(d_pre_b, w["fc1"][:, cols])
        d_hidden = term if d_hidden is None else d_hidden + term
    d_norm, grads[5], grads[6] = norm_grad(d_hidden, kept["n2"][...], kept["r2"][:, :1], gain_two)
    d_mid = dout + d_norm
    d_mid_b = d_mid.astype(BF16)
    grads[4] = jnp.sum(d_mid, axis=0, keepdims=True)
    pack_matrix(staging, dot_tn(kept["att"][...], d_mid_b), BASE_OUT, PITCH_OUT, 0)
    datt_ref[...] = dot_nt(d_mid_b, w["out"][...]).astype(BF16)
    dbias_ref[...] = jnp.zeros_like(dbias_ref)
    vec_rows[0:16, :] = jnp.zeros((16, C), F32)
    scale = HEAD_DIM ** (-0.5)

    @pl.loop(0, NWIN)
    def _(win):
        pair, even, odd, pair_f = pair_masks()
        even_lane = lane_ids((1, LANES)) < WPAD
        even_col = lane_ids((1, 256)) % 64 < 32
        rows = pl.ds(pl.multiple_of(win * WPAD, WPAD), WPAD)
        for g in range(2):
            cols = slice(g * 256, (g + 1) * 256)
            query = stack_pairs(kept["q"][rows, cols], pair)
            key = stack_halves(kept["k"][rows, cols], even, odd)
            value = stack_halves(kept["v"][rows, cols], even, odd)
            d_att = stack_pairs(datt_ref[rows, cols], pair)
            probs = kept["p"][win * 2 + g]
            d_probs = dot_nt(d_att, value)
            left, right = half_sum(d_probs * probs, even_lane)
            d_scores = probs * (d_probs - jnp.where(even_lane, left, right))
            dbias_ref[cols, :] += d_scores
            d_scores_b = d_scores.astype(BF16)
            d_query = gather_pairs(dot(d_scores_b, key), pair_f) * scale
            d_key = dot_tn(d_scores_b, query)
            d_value = dot_tn(probs.astype(BF16), d_att)
            d_key = jnp.where(even_col, d_key[:WPAD], d_key[WPAD:])
            d_value = jnp.where(even_col, d_value[:WPAD], d_value[WPAD:])
            vec_rows[0:1, cols] += jnp.sum(d_query, axis=0, keepdims=True)
            vec_rows[8:9, cols] += jnp.sum(d_value, axis=0, keepdims=True)
            dqkv_ref[rows, cols] = d_query.astype(BF16)
            dqkv_ref[rows, C + g * 256 : C + (g + 1) * 256] = d_key.astype(BF16)
            dqkv_ref[rows, 2 * C + g * 256 : 2 * C + (g + 1) * 256] = d_value.astype(BF16)

    grads[2] = vec_rows[0:1, :]
    grads[3] = vec_rows[8:9, :]
    d_hidden = None
    for f in range(3):
        cols = slice(f * 512, (f + 1) * 512)
        pack_matrix(staging, dot_tn(kept["h1"][...], dqkv_ref[:, cols]), BASE_QKV, PITCH_QKV, f * 4)
        term = dot_nt(dqkv_ref[:, cols], w["qkv"][:, cols])
        d_hidden = term if d_hidden is None else d_hidden + term
    d_norm, grads[0], grads[1] = norm_grad(d_hidden, kept["n1"][...], kept["r1"][:, :1], gain_one)
    d_in = d_mid + d_norm

    even = lane_ids((8, LANES)) < WPAD
    for a in range(WTOK):
        part = dbias_ref[pl.ds(a, 8, stride=WPAD), :]
        part = jnp.concatenate([jnp.where(even, part, 0.0), jnp.where(even, 0.0, part)], axis=0)
        high = part.astype(BF16)
        spread_hi[:, a * LANES : (a + 1) * LANES] = high
        spread_lo[:, a * LANES : (a + 1) * LANES] = (part - high.astype(F32)).astype(BF16)
    g_table = dot_nt(offsets_ref[...], spread_hi[...]) + dot_nt(offsets_ref[...], spread_lo[...])
    g_lanes = dot(g_table.astype(BF16), heads_ref[...]) * lane_mask_ref[...].astype(F32)
    g_rows = dot_tn(rows_ref[...], g_lanes.astype(BF16))
    tail_rows = device_count * shard_rows - BASE_TAIL
    staging[BASE_TAIL : BASE_TAIL + tail_rows, :] = jnp.zeros((tail_rows, LANES), F32)
    staging[BASE_TAIL : BASE_TAIL + 24, :] = g_rows
    lines = []
    for v in range(8):
        lines += [grads[v][:, i * LANES : (i + 1) * LANES] for i in range(4)]
    for part in g_b1:
        lines += [part[:, i * LANES : (i + 1) * LANES] for i in range(4)]
    rolled = pltpu.roll(jnp.concatenate(lines, axis=0), VEC_SKIP, 1)
    first = lane_ids((VEC_ROWS, LANES)) < VEC_SKIP
    low = BASE_TAIL + TAIL_VEC
    staging[low : low + VEC_ROWS, :] += jnp.where(first, 0.0, rolled)
    staging[low + 1 : low + 1 + VEC_ROWS, :] += jnp.where(first, rolled, 0.0)
    return d_in


KEPT = {
    "n1": ((ROWS, C), F32),
    "r1": ((ROWS, LANES), F32),
    "h1": ((ROWS, C), BF16),
    "q": ((ROWS, C), BF16),
    "k": ((ROWS, C), BF16),
    "v": ((ROWS, C), BF16),
    "p": ((2 * NWIN, 256, LANES), F32),
    "att": ((ROWS, C), BF16),
    "n2": ((ROWS, C), F32),
    "r2": ((ROWS, LANES), F32),
    "h2": ((ROWS, C), BF16),
    "slope": ((ROWS, FF), F32),
    "act": ((ROWS, FF), BF16),
}
WEIGHTS = {
    "qkv": ((C, 3 * C), BF16),
    "out": ((C, C), BF16),
    "fc1": ((C, FF), BF16),
    "fc2": ((FF, C), BF16),
}
BACK_SCRATCH = [
    pltpu.VMEM((ROWS, C), BF16),
    pltpu.VMEM((ROWS, 3 * C), BF16),
    pltpu.VMEM((512, LANES), F32),
    pltpu.VMEM((16, WTOK * LANES), BF16),
    pltpu.VMEM((16, WTOK * LANES), BF16),
    pltpu.VMEM((16, C), F32),
]


def unpack_weights(pieces, buffer, sems, staging, w, place, dims):
    sizes, shard_rows, padded_rows, cut = dims
    fetch_pieces(pieces, buffer, sems, sizes, cut)
    flat_to_staging(buffer, staging, place, math.prod(sizes), shard_rows)
    unpack_matrix(staging, w["qkv"], BASE_QKV, PITCH_QKV, 128)
    unpack_matrix(staging, w["out"], BASE_OUT, PITCH_OUT, 128)
    unpack_matrix(staging, w["fc1"], BASE_FC1, PITCH_FC1, 128)
    unpack_matrix(staging, w["fc2"], BASE_FC2, PITCH_FC2, 256)


def first_kernel(dims, *refs):
    place, *pieces = refs[:9]
    images, order, mask, rows_c, lane_c, heads_c, offsets = refs[9:16]
    names = list(KEPT) + list(WEIGHTS)
    stream, vec_out, *outs = refs[16 : 18 + len(names)]
    staging, shift, bias, buffer, sems = refs[18 + len(names) :]
    kept = dict(zip(names, outs))
    unpack_weights(pieces, buffer, sems, staging, kept, place[0], dims)
    vec, b_fc1 = unpack_tail(staging, shift, None)
    vec_out[...] = jnp.concatenate(vec, axis=0)
    build_bias(staging, rows_c, lane_c, heads_c, offsets, bias)
    x = select_rows(order[...], images[...])
    stream[...] = block_forward(x, kept, vec, b_fc1, bias, mask, kept)


def second_kernel(dims, *refs):
    sizes, shard_rows, padded_rows, _ = dims
    device_count = math.prod(sizes)
    valid, place, *pieces = refs[:10]
    stream, cotangent, order, between, mask, rows_c, lane_c, heads_c, offsets = refs[10:19]
    block_out, d_stream, keep, send = refs[19:23]
    names = list(KEPT) + list(WEIGHTS)
    kept = dict(zip(names, refs[23 : 23 + len(names)]))
    staging, shift, bias, buffer, sems, *scratch = refs[23 + len(names) :]
    unpack_weights(pieces, buffer, sems, staging, kept, place[0], dims)
    vec, b_fc1 = unpack_tail(staging, shift, None)
    build_bias(staging, rows_c, lane_c, heads_c, offsets, bias)
    factor = (valid[0] > 0).astype(F32)
    x = select_rows(between[...], stream[...])
    result = block_forward(x, kept, vec, b_fc1, bias, mask, kept)
    back = order[...].T
    block_out[...] = select_rows(back, result)[:IMG_TOK] * factor
    dout = select_rows(order[...], cotangent[...]) * factor
    d_in = block_backward(
        dout, kept, vec[0], vec[5], kept, staging, (rows_c, lane_c, heads_c, offsets), scratch,
        device_count, shard_rows,
    )
    d_stream[...] = select_rows(between[...].T, d_in)
    staging_to_flat(staging, keep, send, place[0], device_count, shard_rows, padded_rows)


def third_kernel(dims, *refs):
    sizes, shard_rows, padded_rows, _ = dims
    device_count = math.prod(sizes)
    valid, place, d_stream, vec, order, rows_c, lane_c, heads_c, offsets = refs[:9]
    names = list(KEPT) + list(WEIGHTS)
    kept = dict(zip(names, refs[9 : 9 + len(names)]))
    input_grad, keep, send = refs[9 + len(names) : 12 + len(names)]
    staging, *scratch = refs[12 + len(names) :]
    factor = (valid[0] > 0).astype(F32)
    d_in = block_backward(
        d_stream[...], kept, vec[0:1, :], vec[5:6, :], kept, staging,
        (rows_c, lane_c, heads_c, offsets), scratch, device_count, shard_rows,
    )
    input_grad[...] = select_rows(order[...].T, d_in)[:IMG_TOK] * factor
    staging_to_flat(staging, keep, send, place[0], device_count, shard_rows, padded_rows)


ANY_SPEC = pl.BlockSpec(memory_space=pl.ANY)
VMEM_SPEC = pl.BlockSpec(memory_space=pltpu.VMEM)
SMEM_SPEC = pl.BlockSpec(memory_space=pltpu.SMEM)
PARAMS = pltpu.CompilerParams(vmem_limit_bytes=60 * 1024 * 1024)


def shapes_of(table):
    return [jax.ShapeDtypeStruct(shape, kind) for shape, kind in table.values()]


def scratch_of(table):
    return [pltpu.VMEM(shape, kind) for shape, kind in table.values()]


def axes_of(mesh):
    devices = list(mesh.devices.flat)
    coords = np.array([tuple(d.coords) + (d.core_on_chip,) for d in devices])
    extent = coords.max(axis=0) - coords.min(axis=0) + 1
    return int(extent[2]), int(extent[1]), int(extent[0]), int(extent[3])


AXES = ("z", "y", "x", "c")


def swap(values, axis, size, step):
    return lax.ppermute(values, axis, [(i, i ^ step) for i in range(size)])


def bits_of(size):
    return [1 << b for b in range(size.bit_length() - 1)]


def after(values, *others):
    return lax.optimization_barrier((values,) + others)[0]


class Gather:
    def __init__(self, shard, sizes, cut):
        self.sizes, self.cut = sizes, cut
        self.whole = shard.reshape((1, 1, 1) + shard.shape)

    def grow(self, values, name, step):
        dim = AXES.index(name)
        got = swap(values, name, self.sizes[dim], step)
        count = values.shape[dim]
        shape = values.shape[:dim] + (count, 1) + values.shape[dim + 1 :]
        joined = jnp.concatenate([values.reshape(shape), got.reshape(shape)], axis=dim + 1)
        return joined.reshape(values.shape[:dim] + (count * 2,) + values.shape[dim + 1 :]), got

    def along_z(self, gate=None):
        for at, step in enumerate(reversed(bits_of(self.sizes[0]))):
            if gate is not None and at < len(gate):
                self.whole = after(self.whole, gate[at])
            self.whole, got = self.grow(self.whole, "z", step)
            yield got

    def split(self):
        self.first = self.whole[..., : self.cut, :]
        self.second = self.whole[..., self.cut :, :]

    def across(self):
        z, y, x, c = self.sizes
        for step in reversed(bits_of(x)):
            self.first, got_first = self.grow(self.first, "x", step)
        for step in reversed(bits_of(y)):
            self.second, got_second = self.grow(self.second, "y", step)
        for step in reversed(bits_of(y)[1:]):
            self.first, got_first = self.grow(self.first, "y", step)
        for step in reversed(bits_of(x)[1:]):
            self.second, got_second = self.grow(self.second, "x", step)
        return got_first, got_second

    def last(self):
        z, y, x, c = self.sizes
        return swap(self.first, "y", y, 1), swap(self.second, "x", x, 1)


def reduce_core(keep, sent, sizes):
    return keep, swap(sent, "c", sizes[3], 1)


def shed(values, got, dim, name, size, step):
    total = values if got is None else values + got
    span = total.shape[dim]
    shaped = total.reshape(total.shape[:dim] + (span // 2, 2) + total.shape[dim + 1 :])
    mine = lax.index_in_dim(shaped, 0, dim + 1, keepdims=False)
    theirs = lax.index_in_dim(shaped, 1, dim + 1, keepdims=False)
    return mine, swap(theirs, name, size, step)


def adam_update(weights_now, grads_now, moment_one, moment_two):
    new_one = BETA_FIRST * moment_one + (1.0 - BETA_FIRST) * grads_now
    new_two = BETA_SECOND * moment_two + (1.0 - BETA_SECOND) * grads_now * grads_now
    corr_one = 1.0 - BETA_FIRST**STEP
    corr_two = 1.0 - BETA_SECOND**STEP
    update = new_one / corr_one / (jnp.sqrt(new_two / corr_two) + EPS_ADAM)
    return (weights_now - LEARN_RATE * (update + WEIGHT_DECAY * weights_now), new_one, new_two)


def local(sizes, images, counts, cotangent, params, first_moment, second_moment):
    device_count = math.prod(sizes)
    shard_len = params.shape[1]
    shard_rows = shard_len // LANES
    padded_rows = round_up(shard_rows, 16)
    flat_rows = device_count * shard_rows

    take_first, take_second = order_matrices()
    order_first = jnp.asarray(take_first[:, :], BF16)
    order_second = jnp.asarray(take_second, BF16)
    between = jnp.asarray(take_second @ take_first.T, BF16)
    masks = key_masks()
    mask_first, mask_second = jnp.asarray(masks[0]), jnp.asarray(masks[1])
    consts = [jnp.asarray(a, BF16) for a in table_constants()] + [offset_lanes()]

    cut = padded_rows // 2 // 16 * 16
    dims = (sizes, shard_rows, padded_rows, cut)
    place = lax.axis_index(AXES).astype(jnp.int32).reshape(1)

    shard = params.astype(BF16).reshape(2, shard_rows, LANES)
    shard = jnp.pad(shard, ((0, 0), (0, padded_rows - shard_rows), (0, 0)))
    one, two = Gather(shard[0], sizes, cut), Gather(shard[1], sizes, cut)
    gates = []
    for got in one.along_z():
        gates.append(got)
    two.whole = after(two.whole, gates[-1])
    one.split()
    across_one = one.across()
    steps_two = two.along_z([gates[-1], across_one[0]])
    for _ in steps_two:
        pass
    two.split()
    last_one = one.last()
    early_one = (swap(one.first, "c", 2, 1), swap(one.second, "c", 2, 1))
    late_one = tuple(swap(v, "c", 2, 1) for v in last_one)
    pieces_one = [one.first, last_one[0], one.second, last_one[1], early_one[0], late_one[0], early_one[1], late_one[1]]
    two.first = after(two.first, last_one[0])
    two.second = after(two.second, last_one[1])
    two.across()
    last_two = two.last()
    early_two = (swap(two.first, "c", 2, 1), swap(two.second, "c", 2, 1))
    late_two = tuple(swap(v, "c", 2, 1) for v in last_two)
    pieces_two = [two.first, last_two[0], two.second, last_two[1], early_two[0], late_two[0], early_two[1], late_two[1]]

    pad_tokens = ((0, ROWS - IMG_TOK), (0, 0))
    image_rows = jnp.pad(images.reshape(IMG_TOK, C), pad_tokens)
    cot_rows = jnp.pad(cotangent.reshape(IMG_TOK, C), pad_tokens)

    half_shape = jax.ShapeDtypeStruct((device_count // 2, padded_rows, LANES), BF16)
    names = len(KEPT) + len(WEIGHTS)
    staging = pltpu.VMEM((flat_rows, LANES), F32)
    copy_count = 2 * sum(math.prod(p.shape[1:3]) for p in pieces_one[:4])
    common = [
        staging,
        pltpu.VMEM((96, LANES), F32),
        pltpu.VMEM((512, LANES), F32),
        pltpu.VMEM((device_count, padded_rows, LANES), BF16),
        pltpu.SemaphoreType.DMA((copy_count,)),
    ]
    stream, vec, *kept = pl.pallas_call(
        functools.partial(first_kernel, dims),
        out_shape=[
            jax.ShapeDtypeStruct((ROWS, C), F32),
            jax.ShapeDtypeStruct((8, C), F32),
            *shapes_of(KEPT),
            *shapes_of(WEIGHTS),
        ],
        in_specs=[SMEM_SPEC] + [ANY_SPEC] * 8 + [VMEM_SPEC] * 7,
        out_specs=[VMEM_SPEC] * (2 + names),
        scratch_shapes=common,
        compiler_params=PARAMS,
        name="first",
    )(place, *pieces_one, image_rows, order_first, mask_first, *consts)

    block_out, d_stream, keep_two, send_two = pl.pallas_call(
        functools.partial(second_kernel, dims),
        out_shape=[
            jax.ShapeDtypeStruct((IMG_TOK, C), F32),
            jax.ShapeDtypeStruct((ROWS, C), F32),
            half_shape,
            half_shape,
        ],
        in_specs=[SMEM_SPEC] * 2 + [ANY_SPEC] * 8 + [VMEM_SPEC] * 9,
        out_specs=[VMEM_SPEC] * 4,
        scratch_shapes=scratch_of(KEPT) + scratch_of(WEIGHTS) + common + BACK_SCRATCH,
        compiler_params=PARAMS,
        name="second",
    )(counts, place, *pieces_two, stream, cot_rows, order_second, between, mask_second, *consts)

    z, y, x, c = sizes

    def begin(keep, sent):
        got = swap(sent, "c", c, 1)
        shape = (z, y, x, padded_rows, LANES)
        keep, got = keep.reshape(shape), got.reshape(shape)
        top = shed(keep[..., :cut, :], got[..., :cut, :], 2, "x", x, 1)
        low = shed(keep[..., cut:, :], got[..., cut:, :], 1, "y", y, 1)
        return top, low

    def finish(top, low):
        for step in bits_of(x)[1:]:
            top = shed(*top, 2, "x", x, step)
        for step in bits_of(y)[1:]:
            low = shed(*low, 1, "y", y, step)
        for step in bits_of(y):
            top = shed(*top, 1, "y", y, step)
        for step in bits_of(x):
            low = shed(*low, 2, "x", x, step)
        both = tuple(jnp.concatenate([a, b], axis=3) for a, b in zip(top, low))
        for step in bits_of(z):
            both = shed(*both, 0, "z", z, step)
        mine, got = both
        return (mine.astype(F32) + got.astype(F32)).reshape(padded_rows, LANES)

    top_two, low_two = begin(keep_two, send_two)
    d_stream = after(d_stream, top_two[0], low_two[0])
    input_grad, keep_one, send_one = pl.pallas_call(
        functools.partial(third_kernel, dims),
        out_shape=[jax.ShapeDtypeStruct((IMG_TOK, C), F32), half_shape, half_shape],
        in_specs=[SMEM_SPEC] * 2 + [VMEM_SPEC] * (7 + names),
        out_specs=[VMEM_SPEC] * 3,
        scratch_shapes=[staging] + BACK_SCRATCH,
        compiler_params=PARAMS,
        name="third",
    )(counts, place, d_stream, vec, order_first, *consts, *kept)
    top_one, low_one = begin(keep_one, send_one)
    sum_two = finish(top_two, low_two)
    sum_one = finish(top_one, low_one)
    param_grads = jnp.stack([sum_one[:shard_rows], sum_two[:shard_rows]])
    param_grads = param_grads.reshape(2, shard_len)
    new_params, new_first, new_second = adam_update(params, param_grads, first_moment, second_moment)
    return (
        block_out.reshape(1, IMG_TOK, C),
        input_grad.reshape(1, IMG_TOK, C),
        param_grads,
        new_params,
        new_first,
        new_second,
    )


def solution(mesh):
    sizes = axes_of(mesh)
    axes = AXES
    fine = Mesh(mesh.devices.reshape(sizes), axes)
    return jax.shard_map(
        functools.partial(local, sizes),
        mesh=fine,
        in_specs=(
            P(axes, None, None),
            P(axes),
            P(axes, None, None),
            P(None, axes),
            P(None, axes),
            P(None, axes),
        ),
        out_specs=(
            P(axes, None, None),
            P(axes, None, None),
            P(None, axes),
            P(None, axes),
            P(None, axes),
            P(None, axes),
        ),
        check_vma=False,
    )
```
